32 devices in a mesh: dp: 4 (over y, x), ctx: 2 (over core), tp: 4 (over z).
Axes of the slice: x: 2, y: 2, z: 4, core: 2. Of those that a mesh axis runs over, the one named last changes fastest.
Arguments:
- tokens: bfloat16 [4, 512, 1024], P('dp', 'ctx'), may hold values from -6 to 6
- segments: int32 [4, 512], P('dp'), may hold values from 0 to 2, never falling along the last dimension, each value on 1 to 384 neighbouring positions
- cotangent: bfloat16 [4, 512, 1024], P('dp', 'ctx'), may hold values from -6 to 6
- mixer_gain: bfloat16 [1024], P(('dp', 'ctx')), may hold values from 0.5 to 1.5
- mlp_gain: bfloat16 [1024], P(('dp', 'ctx')), may hold values from 0.5 to 1.5
- query_weight: bfloat16 [1024, 1024], P(('dp', 'ctx'), 'tp'), may hold values from -0.1875 to 0.1875
- key_weight: bfloat16 [1024, 1024], P(('dp', 'ctx'), 'tp'), may hold values from -0.1875 to 0.1875
- value_weight: bfloat16 [1024, 2048], P(('dp', 'ctx'), 'tp'), may hold values from -0.1875 to 0.1875
- gate_weight: bfloat16 [1024, 2048], P(('dp', 'ctx'), 'tp'), may hold values from -0.1875 to 0.1875
- decay_weight: bfloat16 [1024, 8], P(('dp', 'ctx'), 'tp'), may hold values from -0.1875 to 0.1875
- beta_weight: bfloat16 [1024, 8], P(('dp', 'ctx'), 'tp'), may hold values from -0.1875 to 0.1875
- output_weight: bfloat16 [1024, 2048], P(('dp', 'ctx'), 'tp'), may hold values from -0.125 to 0.125
- conv_query: float32 [4, 1024], P(None, 'tp'), may hold values from -3 to 3
- conv_key: float32 [4, 1024], P(None, 'tp'), may hold values from -3 to 3
- conv_value: float32 [4, 2048], P(None, 'tp'), may hold values from -3 to 3
- decay_log: float32 [8], P('tp'), may hold values from -7 to -3
- decay_bias: float32 [8], P('tp'), may hold values from -2 to 1
- head_gain: float32 [256], replicated, may hold values from 0.5 to 1.5
- hidden_gate: bfloat16 [1024, 2816], P(('dp', 'ctx'), 'tp'), may hold values from -0.1875 to 0.1875
- hidden_up: bfloat16 [1024, 2816], P(('dp', 'ctx'), 'tp'), may hold values from -0.1875 to 0.1875
- hidden_down: bfloat16 [1024, 2816], P(('dp', 'ctx'), 'tp'), may hold values from -0.109375 to 0.109375
Outputs:
- block_out: bfloat16 [4, 512, 1024], P('dp', 'ctx')
- tokens_grad: float32 [4, 512, 1024], P('dp', 'ctx')
- mixer_gain_grad: float32 [1024], P(('dp', 'ctx'))
- mlp_gain_grad: float32 [1024], P(('dp', 'ctx'))
- query_grad: float32 [1024, 1024], P(('dp', 'ctx'), 'tp')
- key_grad: float32 [1024, 1024], P(('dp', 'ctx'), 'tp')
- value_grad: float32 [1024, 2048], P(('dp', 'ctx'), 'tp')
- gate_grad: float32 [1024, 2048], P(('dp', 'ctx'), 'tp')
- decay_grad: float32 [1024, 8], P(('dp', 'ctx'), 'tp')
- beta_grad: float32 [1024, 8], P(('dp', 'ctx'), 'tp')
- output_grad: float32 [1024, 2048], P(('dp', 'ctx'), 'tp')
- conv_query_grad: float32 [4, 1024], P(None, 'tp')
- conv_key_grad: float32 [4, 1024], P(None, 'tp')
- conv_value_grad: float32 [4, 2048], P(None, 'tp')
- decay_log_grad: float32 [8], P('tp')
- decay_bias_grad: float32 [8], P('tp')
- head_gain_grad: float32 [256], replicated
- hidden_gate_grad: float32 [1024, 2816], P(('dp', 'ctx'), 'tp')
- hidden_up_grad: float32 [1024, 2816], P(('dp', 'ctx'), 'tp')
- hidden_down_grad: float32 [1024, 2816], P(('dp', 'ctx'), 'tp')
The draws below stay inside these ranges and needn't reach their ends.
Inputs may be any that keep to these rules, and one draw needn't show every extreme that they name: `segments`: along each sequence the numbers start at 0, never fall and rise by one at each document's first token; every document has 1 to 384 tokens and one has exactly 384.
All inputs are finite; a program needn't handle non-finite values.
Results may differ from the reference program's by a relative error of at most 0.014.
The reference program's roundings to bfloat16 on the way count: a program that leaves them out, or rounds other values in their place, can miss the bound.
Values may be sent and summed in bfloat16 or wider, within the bound.
A program may use at most 128 MiB of HBM per device.

```python
import math
from functools import partial
import jax
import jax.numpy as jnp
import numpy as np
from jax import lax

D = 1024
HEADS = 8
KEY_DIM = 128
VALUE_DIM = 256
FF = 2816
CONV = 4
GROUP = 64
SEQ_LEN = 512
SEQS = 4
DOCS = 3
DOC_MOST = 384


def shard_levels(key, dims, split, smallest, high):
    loudness = 1.0
    for dim, parts in split:
        heights = jax.random.uniform(jax.random.fold_in(jax.random.fold_in(key, 6), dim), (parts,), jnp.float32, smallest / len(split), high / len(split))
        loudness = loudness * jnp.repeat(jnp.exp(heights), dims[dim] // parts).reshape((-1,) + (1,) * (len(dims) - 1 - dim))
    return loudness


def split_up(count, total, limit, slope):
    portions = [(1 << 20) // math.isqrt(grade ** slope) + 1 for grade in range(2, count + 1)]
    surplus, counts = total - limit - (count - 1), [1] * (count - 1)
    while surplus > 0:
        candidates = [i for i in range(count - 1) if counts[i] < limit]
        whole, budget = sum([portions[i] for i in candidates]), surplus
        for i in candidates:
            addition = min(limit - counts[i], max(1, budget * portions[i] // whole), surplus)
            counts[i] = counts[i] + addition
            surplus = surplus - addition
    return np.array([limit] + counts)


def uneven_parts(rng, amount, total, limit, lean):
    if amount == 2:
        one = jax.random.randint(rng, (), max(1, total - limit), min(limit, total - 1) + 1)
        return jnp.stack([one, total - one])
    sizes = jnp.asarray(split_up(amount, total, limit, lean), jnp.int32)
    pairs = (amount - 1) // 2
    donor, receiver = sizes[1:1 + 2 * pairs:2], sizes[2:2 + 2 * pairs:2]
    room = jnp.minimum(donor - 1, limit - receiver)
    moved = jax.random.randint(jax.random.fold_in(rng, 1), (pairs,), 0, 1 << 20) % (room + 1)
    sizes = sizes.at[1:1 + 2 * pairs:2].set(donor - moved).at[2:2 + 2 * pairs:2].set(receiver + moved)
    return sizes[jax.random.permutation(jax.random.fold_in(rng, 2), amount)]


def bell_draw(stream_key, dims, scale, limit, cuts=(), held_as=jnp.bfloat16):
    level = shard_levels(stream_key, dims, cuts, -0.22, 0.18) if cuts else 1.0
    values = jax.random.normal(stream_key, dims, jnp.float32) * scale * level
    return jnp.minimum(jnp.maximum(values, -limit), limit).astype(held_as)


def setup_inputs(seed: int = 0) -> dict:
    arg_keys = jax.random.split(jax.random.key(seed), 22)
    tokens = bell_draw(arg_keys[0], (SEQS, SEQ_LEN, D), 1.0, 6.0, ((0, 4), (1, 2)))
    segments = jax.vmap(lambda own: jnp.searchsorted(jnp.cumsum(uneven_parts(own, DOCS, SEQ_LEN, DOC_MOST, 2)), jnp.arange(SEQ_LEN), side="right"))(jax.random.split(arg_keys[1], SEQS)).reshape((SEQS, SEQ_LEN)).astype(jnp.int32)
    cotangent = bell_draw(arg_keys[2], (SEQS, SEQ_LEN, D), 1.0, 6.0, ((0, 4), (1, 2)))
    mixer_gain = jnp.clip(1.0 + 0.1 * jax.random.normal(arg_keys[3], (D,), jnp.float32), 0.5, 1.5).astype(jnp.bfloat16)
    mlp_gain = jnp.clip(1.0 + 0.1 * jax.random.normal(arg_keys[4], (D,), jnp.float32), 0.5, 1.5).astype(jnp.bfloat16)
    query_weight = bell_draw(arg_keys[5], (D, HEADS * KEY_DIM), D ** -0.5, 0.1875, ((0, 8), (1, 4)))
    key_weight = bell_draw(arg_keys[6], (D, HEADS * KEY_DIM), D ** -0.5, 0.1875, ((0, 8), (1, 4)))
    value_weight = bell_draw(arg_keys[7], (D, HEADS * VALUE_DIM), D ** -0.5, 0.1875, ((0, 8), (1, 4)))
    gate_weight = bell_draw(arg_keys[8], (D, HEADS * VALUE_DIM), D ** -0.5, 0.1875, ((0, 8), (1, 4)))
    decay_weight = bell_draw(arg_keys[9], (D, HEADS), D ** -0.5, 0.1875, ((0, 8), (1, 4)))
    beta_weight = bell_draw(arg_keys[10], (D, HEADS), D ** -0.5, 0.1875, ((0, 8), (1, 4)))
    output_weight = bell_draw(arg_keys[11], (D, HEADS * VALUE_DIM), (HEADS * VALUE_DIM) ** -0.5, 0.125, ((0, 8), (1, 4)))
    conv_query = bell_draw(arg_keys[12], (CONV, HEADS * KEY_DIM), CONV ** -0.5, 3.0, ((1, 4),), jnp.float32)
    conv_key = bell_draw(arg_keys[13], (CONV, HEADS * KEY_DIM), CONV ** -0.5, 3.0, ((1, 4),), jnp.float32)
    conv_value = bell_draw(arg_keys[14], (CONV, HEADS * VALUE_DIM), CONV ** -0.5, 3.0, ((1, 4),), jnp.float32)
    decay_log = jnp.clip(-7.0 + 4.0 * jax.random.uniform(arg_keys[15], (HEADS,), jnp.float32) ** shard_levels(arg_keys[15], (HEADS,), ((0, 4),), -0.2, 0.2), -7.0, -3.0)
    decay_bias = jnp.clip(-2.0 + 3.0 * jax.random.uniform(arg_keys[16], (HEADS,), jnp.float32) ** shard_levels(arg_keys[16], (HEADS,), ((0, 4),), -0.2, 0.2), -2.0, 1.0)
    head_gain = jnp.clip(1.0 + 0.1 * jax.random.normal(arg_keys[17], (VALUE_DIM,), jnp.float32), 0.5, 1.5)
    hidden_gate = bell_draw(arg_keys[18], (D, FF), D ** -0.5, 0.1875, ((0, 8), (1, 4)))
    hidden_up = bell_draw(arg_keys[19], (D, FF), D ** -0.5, 0.1875, ((0, 8), (1, 4)))
    hidden_down = bell_draw(arg_keys[20], (D, FF), FF ** -0.5, 0.109375, ((0, 8), (1, 4)))
    return dict(tokens=tokens, segments=segments, cotangent=cotangent, mixer_gain=mixer_gain, mlp_gain=mlp_gain, query_weight=query_weight, key_weight=key_weight, value_weight=value_weight, gate_weight=gate_weight, decay_weight=decay_weight, beta_weight=beta_weight, output_weight=output_weight, conv_query=conv_query, conv_key=conv_key, conv_value=conv_value, decay_log=decay_log, decay_bias=decay_bias, head_gain=head_gain, hidden_gate=hidden_gate, hidden_up=hidden_up, hidden_down=hidden_down)


EPSILON = 1e-06
HIGHEST = lax.Precision.HIGHEST

def features(pre_ext, seg_ext, conv_weight, decay_lin, beta_lin, decay_log, decay_bias, key_dim):
    margin = conv_weight.shape[0] - 1
    row_count = pre_ext.shape[0] - margin
    head_count = decay_lin.shape[1]
    own_segment = seg_ext[margin:]
    convolved = jnp.zeros((row_count, pre_ext.shape[1]), jnp.float32)
    for lag in range(margin + 1):
        first_row = margin - lag
        same_doc = (seg_ext[first_row:first_row + row_count] == own_segment).astype(jnp.float32)
        convolved = convolved + conv_weight[lag][None, :] * pre_ext[first_row:first_row + row_count] * same_doc[:, None]
    activated = jax.nn.silu(convolved)
    query_cols = head_count * key_dim
    queries = activated[:, :query_cols].reshape(row_count, head_count, key_dim)
    key_rows = activated[:, query_cols:2 * query_cols].reshape(row_count, head_count, key_dim)
    value_rows = activated[:, 2 * query_cols:].reshape(row_count, head_count, -1)
    queries = queries * lax.rsqrt(lax.optimization_barrier(jnp.sum(queries * queries, -1, keepdims=True)) + EPSILON) * key_dim ** (-0.5)
    key_rows = key_rows * lax.rsqrt(lax.optimization_barrier(jnp.sum(key_rows * key_rows, -1, keepdims=True)) + EPSILON)
    decay_rate = -jnp.exp(decay_log)[None, :] * jax.nn.softplus(decay_lin + decay_bias[None, :])
    beta_gate = jax.nn.sigmoid(beta_lin)
    starts = (own_segment != seg_ext[margin - 1:margin - 1 + row_count]).astype(jnp.float32)
    return (queries, key_rows, value_rows, decay_rate, beta_gate, starts)

def unit_lower_inverse(lower_part):
    order = lower_part.shape[-1]
    negated = -lower_part
    inverse = jnp.eye(order, dtype=jnp.float32)[None] + negated
    power = negated
    span = 2
    while span < order:
        power = jnp.einsum('hij,hjk->hik', power, power, precision=HIGHEST)
        inverse = inverse + jnp.einsum('hij,hjk->hik', inverse, power, precision=HIGHEST)
        span = span * 2
    return inverse

def group_update(memory, inputs):
    queries, key_rows, value_rows, decay_rate, beta_gate, starts = inputs
    order = queries.shape[0]
    cumulative = jnp.cumsum(decay_rate, axis=0)
    counted = jnp.cumsum(starts)
    position = jnp.arange(order)
    same_doc = (counted[:, None] == counted[None, :]) & (position[None, :] <= position[:, None])
    strictly = (same_doc & (position[None, :] < position[:, None])).astype(jnp.float32)
    spread = cumulative[:, None, :] - cumulative[None, :, :]
    decay_pair = jnp.exp(jnp.where(same_doc[:, :, None], spread, 0.0)) * same_doc.astype(jnp.float32)[:, :, None]
    anchor = jnp.exp(cumulative) * (counted == 0).astype(jnp.float32)[:, None]
    closing = decay_pair[order - 1]
    key_gram = jnp.einsum('thd,jhd->htj', key_rows, key_rows, precision=HIGHEST)
    lower_part = jnp.transpose(beta_gate)[:, :, None] * jnp.transpose(decay_pair, (2, 0, 1)) * key_gram * strictly[None]
    inverse = unit_lower_inverse(lower_part)
    key_state = jnp.einsum('thd,hdw->thw', key_rows, memory, precision=HIGHEST)
    target = beta_gate[:, :, None] * (value_rows - anchor[:, :, None] * key_state)
    updates = jnp.einsum('htj,jhw->thw', inverse, target, precision=HIGHEST)
    query_state = jnp.einsum('thd,hdw->thw', queries, memory, precision=HIGHEST)
    query_key = jnp.einsum('thd,jhd->tjh', queries, key_rows, precision=HIGHEST) * decay_pair
    output_rows = anchor[:, :, None] * query_state + jnp.einsum('tjh,jhw->thw', query_key, updates, precision=HIGHEST)
    new_memory = anchor[order - 1][:, None, None] * memory + jnp.einsum('jhd,jhw->hdw', key_rows * closing[:, :, None], updates, precision=HIGHEST)
    return (new_memory, output_rows)

def delta_run(queries, key_rows, value_rows, decay_rate, beta_gate, starts, memory, group):
    row_count = queries.shape[0]
    blocks = row_count // group
    pieces = tuple((member.reshape((blocks, group) + member.shape[1:]) for member in (queries, key_rows, value_rows, decay_rate, beta_gate, starts)))
    last_memory, outputs = lax.scan(group_update, memory, pieces)
    return (last_memory, outputs.reshape((row_count,) + outputs.shape[2:]))

def gated(output_rows, gate_lin, head_gain):
    row_count, head_count, value_dim = output_rows.shape
    scaled = output_rows * lax.rsqrt(lax.optimization_barrier(jnp.mean(output_rows * output_rows, -1, keepdims=True)) + EPSILON)
    gate_rows = gate_lin.reshape(row_count, head_count, value_dim)
    return (scaled * head_gain * jax.nn.silu(gate_rows)).reshape(row_count, head_count * value_dim)

def mixer(pre_ext, gate_lin, decay_lin, beta_lin, conv_weight, decay_log, decay_bias, head_gain, seg_ext, key_dim, group):
    queries, key_rows, value_rows, decay_rate, beta_gate, starts = features(pre_ext, seg_ext, conv_weight, decay_lin, beta_lin, decay_log, decay_bias, key_dim)
    memory = jnp.zeros((decay_lin.shape[1], key_dim, value_rows.shape[2]), jnp.float32)
    last_memory, output_rows = delta_run(queries, key_rows, value_rows, decay_rate, beta_gate, starts, memory, group)
    return gated(output_rows, gate_lin, head_gain)

def reference(tokens, segments, cotangent, mixer_gain, mlp_gain, query_weight, key_weight, value_weight, gate_weight, decay_weight, beta_weight, output_weight, conv_query, conv_key, conv_value, decay_log, decay_bias, head_gain, hidden_gate, hidden_up, hidden_down):
    in_weights = jnp.concatenate([query_weight, key_weight, value_weight, gate_weight, decay_weight, beta_weight], 1)
    conv_weight = jnp.concatenate([conv_query, conv_key, conv_value], 1)
    query_cols = HEADS * KEY_DIM
    value_cols = HEADS * VALUE_DIM
    conv_cols = 2 * query_cols + value_cols
    margin = CONV - 1
    gain_one = mixer_gain.astype(jnp.float32)
    gain_two = mlp_gain.astype(jnp.float32)

    def one_sequence(items):
        token_rows, seg_row, grad_rows = items
        inputs = token_rows.astype(jnp.float32)
        rms_one = lax.rsqrt(lax.optimization_barrier(jnp.mean(inputs * inputs, -1, keepdims=True)) + EPSILON)
        normed_one = inputs * rms_one
        hidden_one = (normed_one * gain_one).astype(jnp.bfloat16)
        projected = jnp.dot(hidden_one, in_weights, preferred_element_type=jnp.float32)
        pre_conv = projected[:, :conv_cols].astype(jnp.bfloat16)
        gate_lin = projected[:, conv_cols:conv_cols + value_cols]
        decay_lin = projected[:, conv_cols + value_cols:conv_cols + value_cols + HEADS]
        beta_lin = projected[:, conv_cols + value_cols + HEADS:]
        pre_ext = jnp.concatenate([jnp.zeros((margin, conv_cols), jnp.float32), pre_conv.astype(jnp.float32)], 0)
        seg_ext = jnp.concatenate([jnp.full((margin,), -1, jnp.int32), seg_row.astype(jnp.int32)], 0)
        mixer_fn = partial(mixer, seg_ext=seg_ext, key_dim=KEY_DIM, group=GROUP)
        mixed, mixer_back = jax.vjp(mixer_fn, pre_ext, gate_lin, decay_lin, beta_lin, conv_weight, decay_log, decay_bias, head_gain)
        mixed_b = mixed.astype(jnp.bfloat16)
        middle = inputs + jnp.dot(mixed_b, output_weight.T, preferred_element_type=jnp.float32)
        rms_two = lax.rsqrt(lax.optimization_barrier(jnp.mean(middle * middle, -1, keepdims=True)) + EPSILON)
        normed_two = middle * rms_two
        hidden_two = (normed_two * gain_two).astype(jnp.bfloat16)
        gate_pre = jnp.dot(hidden_two, hidden_gate, preferred_element_type=jnp.float32)
        up_pre = jnp.dot(hidden_two, hidden_up, preferred_element_type=jnp.float32)
        sigma = jax.nn.sigmoid(gate_pre)
        swish = gate_pre * sigma
        activ = (swish * up_pre).astype(jnp.bfloat16)
        block_rows = (middle + jnp.dot(activ, hidden_down.T, preferred_element_type=jnp.float32)).astype(jnp.bfloat16)
        grad_out = grad_rows.astype(jnp.float32)
        d_activ = jnp.dot(grad_rows, hidden_down, preferred_element_type=jnp.float32)
        d_gate_pre = (d_activ * up_pre * sigma * (1.0 + gate_pre * (1.0 - sigma))).astype(jnp.bfloat16)
        d_up_pre = (d_activ * swish).astype(jnp.bfloat16)
        grad_down = jnp.dot(grad_rows.T, activ, preferred_element_type=jnp.float32)
        grad_hgate = jnp.dot(hidden_two.T, d_gate_pre, preferred_element_type=jnp.float32)
        grad_hup = jnp.dot(hidden_two.T, d_up_pre, preferred_element_type=jnp.float32)
        d_hidden_two = jnp.dot(d_gate_pre, hidden_gate.T, preferred_element_type=jnp.float32) + jnp.dot(d_up_pre, hidden_up.T, preferred_element_type=jnp.float32)
        grad_gain_two = lax.optimization_barrier(jnp.sum(d_hidden_two * normed_two, 0))
        dn_two = d_hidden_two * gain_two
        d_middle = grad_out + rms_two * (dn_two - normed_two * lax.optimization_barrier(jnp.mean(dn_two * normed_two, -1, keepdims=True)))
        d_middle_b = d_middle.astype(jnp.bfloat16)
        d_mixed = jnp.dot(d_middle_b, output_weight, preferred_element_type=jnp.float32)
        grad_output = jnp.dot(d_middle_b.T, mixed_b, preferred_element_type=jnp.float32)
        d_pre_ext, d_gate, d_decay, d_beta, d_conv, d_log, d_bias, d_head = mixer_back(d_mixed)
        d_proj = jnp.concatenate([d_pre_ext[margin:], d_gate, d_decay, d_beta], 1).astype(jnp.bfloat16)
        grad_input = jnp.dot(hidden_one.T, d_proj, preferred_element_type=jnp.float32)
        d_hidden_one = jnp.dot(d_proj, in_weights.T, preferred_element_type=jnp.float32)
        grad_gain_one = lax.optimization_barrier(jnp.sum(d_hidden_one * normed_one, 0))
        dn_one = d_hidden_one * gain_one
        grad_tokens = d_middle + rms_one * (dn_one - normed_one * lax.optimization_barrier(jnp.mean(dn_one * normed_one, -1, keepdims=True)))
        grads = (grad_gain_one, grad_gain_two, grad_input, grad_output, d_conv, d_log, d_bias, d_head, grad_hgate, grad_hup, grad_down)
        return (block_rows, grad_tokens, grads)
    block_out, tokens_grad, stacked = lax.map(one_sequence, (tokens, segments, cotangent))
    grad_gain_one, grad_gain_two, grad_input, grad_output, d_conv, d_log, d_bias, d_head, grad_hgate, grad_hup, grad_down = tuple((lax.optimization_barrier(jnp.sum(member, 0)) for member in stacked))
    splits = [0, query_cols, 2 * query_cols, conv_cols, conv_cols + value_cols, conv_cols + value_cols + HEADS, conv_cols + value_cols + 2 * HEADS]
    return (block_out, tokens_grad, grad_gain_one, grad_gain_two, grad_input[:, splits[0]:splits[1]], grad_input[:, splits[1]:splits[2]], grad_input[:, splits[2]:splits[3]], grad_input[:, splits[3]:splits[4]], grad_input[:, splits[4]:splits[5]], grad_input[:, splits[5]:splits[6]], grad_output, d_conv[:, :query_cols], d_conv[:, query_cols:2 * query_cols], d_conv[:, 2 * query_cols:], d_log, d_bias, d_head, grad_hgate, grad_hup, grad_down)
```

```python
from functools import partial

import jax
import jax.numpy as jnp
from jax import lax
from jax.sharding import PartitionSpec as P

GROUP = 64


EPSILON = 1e-06
HIGHEST = lax.Precision.HIGHEST
HIGH = lax.Precision.HIGH
LANES = 128


def passed_along(value, axis, by):
    devices = lax.axis_size(axis)
    pairs = [(i, i + by) for i in range(devices) if 0 <= i + by < devices]
    return lax.ppermute(value, axis, pairs)


def features(pre_ext, seg_ext, conv_weight, decay_lin, beta_lin, decay_log, decay_bias, key_dim):
    margin = conv_weight.shape[0] - 1
    row_count = pre_ext.shape[0] - margin
    head_count = decay_lin.shape[1]
    own_segment = seg_ext[margin:]
    convolved = jnp.zeros((row_count, pre_ext.shape[1]), jnp.float32)
    for lag in range(margin + 1):
        first_row = margin - lag
        same_doc = (seg_ext[first_row : first_row + row_count] == own_segment).astype(jnp.float32)
        convolved = (
            convolved
            + conv_weight[lag][None, :]
            * pre_ext[first_row : first_row + row_count]
            * same_doc[:, None]
        )
    activated = jax.nn.silu(convolved)
    query_cols = head_count * key_dim
    queries = activated[:, :query_cols].reshape(row_count, head_count, key_dim)
    key_rows = activated[:, query_cols : 2 * query_cols].reshape(row_count, head_count, key_dim)
    value_rows = activated[:, 2 * query_cols :].reshape(row_count, head_count, -1)
    queries = (
        queries
        * lax.rsqrt(jnp.sum(queries * queries, -1, keepdims=True) + EPSILON)
        * key_dim ** (-0.5)
    )
    key_rows = key_rows * lax.rsqrt(jnp.sum(key_rows * key_rows, -1, keepdims=True) + EPSILON)
    decay_rate = -jnp.exp(decay_log)[None, :] * jax.nn.softplus(decay_lin + decay_bias[None, :])
    beta_gate = jax.nn.sigmoid(beta_lin)
    starts = (own_segment != seg_ext[margin - 1 : margin - 1 + row_count]).astype(jnp.float32)
    return (queries, key_rows, value_rows, decay_rate, beta_gate, starts)


def lower_inverse_value(lower_part):
    order = lower_part.shape[-1]
    negated = -lower_part
    inverse = jnp.eye(order, dtype=jnp.float32)[None] + negated
    power = negated
    span = 2
    while span < order:
        power = jnp.einsum("bij,bjk->bik", power, power, precision=HIGHEST)
        inverse = inverse + jnp.einsum("bij,bjk->bik", inverse, power, precision=HIGHEST)
        span = span * 2
    return inverse


@jax.custom_vjp
def unit_lower_inverse(lower_part):
    return lower_inverse_value(lower_part)


def inverse_forward(lower_part):
    inverse = lower_inverse_value(lower_part)
    return inverse, inverse


def inverse_backward(inverse, grad):
    half = jnp.einsum("bji,bjk->bik", inverse, grad, precision=HIGHEST)
    return (-jnp.einsum("bij,bkj->bik", half, inverse, precision=HIGHEST),)


unit_lower_inverse.defvjp(inverse_forward, inverse_backward)


def mm(spec, left, right):
    return jnp.einsum(spec, left, right, precision=HIGH)


def group_maps(queries, key_rows, value_rows, decay_rate, beta_gate, starts, group):
    row_count, head_count, key_dim = queries.shape
    blocks = row_count // group

    def batched(member):
        tail = member.shape[2:]
        split = member.reshape((blocks, group, head_count) + tail)
        moved = jnp.moveaxis(split, 2, 1)
        return moved.reshape((blocks * head_count, group) + tail)

    queries, key_rows, value_rows = batched(queries), batched(key_rows), batched(value_rows)
    position = jnp.arange(group)
    until = (position[None, :] <= position[:, None]).astype(jnp.float32)
    beta = batched(beta_gate)
    cumulative = jnp.einsum("ts,bs->bt", until, batched(decay_rate), precision=HIGHEST)
    counted = jnp.cumsum(starts.reshape(blocks, group), axis=1)
    counted = jnp.broadcast_to(counted[:, None, :], (blocks, head_count, group))
    counted = counted.reshape(blocks * head_count, group)
    same_doc = (counted[:, :, None] == counted[:, None, :]) & (
        position[None, None, :] <= position[None, :, None]
    )
    same_value = same_doc.astype(jnp.float32)
    strictly = same_value * (position[None, :] < position[:, None]).astype(jnp.float32)[None]
    spread = cumulative[:, :, None] - cumulative[:, None, :]
    decay_pair = jnp.exp(jnp.where(same_doc, spread, 0.0)) * same_value
    anchor = jnp.exp(cumulative) * (counted == 0).astype(jnp.float32)
    closing = decay_pair[:, group - 1, :]
    key_gram = mm("btd,bjd->btj", key_rows, key_rows)
    inverse = unit_lower_inverse(beta[:, :, None] * decay_pair * key_gram * strictly)
    right = beta[:, :, None] * jnp.concatenate([-anchor[:, :, None] * key_rows, value_rows], 2)
    updates = mm("btj,bjw->btw", inverse, right)
    query_key = mm("btd,bjd->btj", queries, key_rows) * decay_pair
    from_rows = mm("btj,bjw->btw", query_key, updates)
    carried = from_rows[:, :, :key_dim] + anchor[:, :, None] * queries
    local_out = from_rows[:, :, key_dim:]
    maps = mm("bjd,bjw->bdw", key_rows * closing[:, :, None], updates)
    last = anchor[:, group - 1]
    transfer = maps[:, :, :key_dim] + last[:, None, None] * jnp.eye(key_dim, dtype=jnp.float32)
    offset = maps[:, :, key_dim:]

    def grouped(member):
        return member.reshape((blocks, head_count) + member.shape[1:])

    return grouped(carried), grouped(local_out), grouped(transfer), grouped(offset)


def compose(carried, local_out, transfer, offset):
    blocks = carried.shape[0]
    key_dim = carried.shape[-1]
    running = jnp.concatenate([transfer[0], offset[0]], 2)
    before = []
    for block in range(1, blocks):
        before.append(running)
        running = mm("hde,hew->hdw", transfer[block], running)
        running = jnp.concatenate(
            [running[:, :, :key_dim], running[:, :, key_dim:] + offset[block]], 2
        )
    if blocks > 1:
        mixed_in = mm("ghtd,ghdw->ghtw", carried[1:], jnp.stack(before))
        carried = jnp.concatenate([carried[:1], mixed_in[..., :key_dim]], 0)
        local_out = jnp.concatenate(
            [local_out[:1], local_out[1:] + mixed_in[..., key_dim:]], 0
        )
    return carried, local_out, running[:, :, :key_dim], running[:, :, key_dim:]


def gated(output_rows, gate_lin, head_gain):
    row_count, head_count, value_dim = output_rows.shape
    scaled = output_rows * lax.rsqrt(
        jnp.mean(output_rows * output_rows, -1, keepdims=True) + EPSILON
    )
    gate_rows = gate_lin.reshape(row_count, head_count, value_dim)
    return (scaled * head_gain * jax.nn.silu(gate_rows)).reshape(row_count, head_count * value_dim)


def expand(
    pre_ext, decay_lin, beta_lin, conv_weight, decay_log, decay_bias, seg_ext, key_dim, group
):
    queries, key_rows, value_rows, decay_rate, beta_gate, starts = features(
        pre_ext, seg_ext, conv_weight, decay_lin, beta_lin, decay_log, decay_bias, key_dim
    )
    return compose(
        *group_maps(queries, key_rows, value_rows, decay_rate, beta_gate, starts, group)
    )


def finish(carried, local_out, initial, gate_lin, head_gain):
    output_rows = local_out + mm("ghtd,hdw->ghtw", carried, initial)
    blocks, head_count, group, value_dim = output_rows.shape
    output_rows = jnp.transpose(output_rows, (0, 2, 1, 3)).reshape(
        blocks * group, head_count, value_dim
    )
    return gated(output_rows, gate_lin, head_gain)


def apply_map(matrix, addend, incoming):
    return mm("hde,hew->hdw", matrix, incoming) + addend


def local(
    tokens,
    segments,
    cotangent,
    mixer_gain,
    mlp_gain,
    query_weight,
    key_weight,
    value_weight,
    gate_weight,
    decay_weight,
    beta_weight,
    output_weight,
    conv_query,
    conv_key,
    conv_value,
    decay_log,
    decay_bias,
    head_gain,
    hidden_gate,
    hidden_up,
    hidden_down,
):
    width = tokens.shape[-1]
    inputs = tokens.reshape(-1, width).astype(jnp.float32)
    row_count = inputs.shape[0]
    query_cols = query_weight.shape[1]
    value_cols = value_weight.shape[1]
    head_count = decay_weight.shape[1]
    ff_cols = hidden_gate.shape[1]
    axes = ("dp", "ctx")
    used = 2 * query_cols + 2 * value_cols + 2 * head_count + 2
    pad_cols = -used % LANES
    own_rows = query_weight.shape[0]
    in_weights = lax.all_gather(
        jnp.concatenate(
            [
                query_weight,
                key_weight,
                value_weight,
                gate_weight,
                decay_weight,
                beta_weight,
                mixer_gain[:, None],
                mlp_gain[:, None],
                jnp.zeros((own_rows, pad_cols), jnp.bfloat16),
            ],
            1,
        ),
        axes,
        axis=0,
        tiled=True,
    )
    full_output = lax.all_gather(output_weight, axes, axis=0, tiled=True)
    full_gate_up = lax.all_gather(
        jnp.concatenate([hidden_gate, hidden_up], 1), axes, axis=0, tiled=True
    )
    full_hidden_down = lax.all_gather(hidden_down, axes, axis=0, tiled=True)
    gain_one = in_weights[:, used - 2].astype(jnp.float32)
    gain_two = in_weights[:, used - 1].astype(jnp.float32)
    conv_cols = 2 * query_cols + value_cols
    key_dim = query_cols // head_count
    rms_one = lax.rsqrt(jnp.mean(inputs * inputs, -1, keepdims=True) + EPSILON)
    normed_one = inputs * rms_one
    hidden_one = (normed_one * gain_one).astype(jnp.bfloat16)
    projected = jnp.dot(hidden_one, in_weights, preferred_element_type=jnp.float32)
    pre_conv = projected[:, :conv_cols].astype(jnp.bfloat16)
    gate_lin = projected[:, conv_cols : conv_cols + value_cols]
    decay_lin = projected[:, conv_cols + value_cols : conv_cols + value_cols + head_count]
    beta_lin = projected[:, used - 2 - head_count : used - 2]
    conv_weight = jnp.concatenate([conv_query, conv_key, conv_value], 1)
    margin = conv_weight.shape[0] - 1
    edge_rows = passed_along(pre_conv[row_count - margin :], "ctx", 1)
    pre_ext = jnp.concatenate([edge_rows, pre_conv], 0).astype(jnp.float32)
    seg_padded = jnp.concatenate([jnp.full((margin,), -1, jnp.int32), segments.reshape(-1)], 0)
    seg_ext = lax.dynamic_slice_in_dim(
        seg_padded, lax.axis_index("ctx") * row_count, row_count + margin
    )
    expand_fn = partial(expand, seg_ext=seg_ext, key_dim=key_dim, group=GROUP)
    (carried, local_out, transfer, offset), expand_back = jax.vjp(
        expand_fn, pre_ext, decay_lin, beta_lin, conv_weight, decay_log, decay_bias
    )

    initial = jnp.zeros_like(offset)
    for _ in range(lax.axis_size("ctx") - 1):
        initial = passed_along(apply_map(transfer, offset, initial), "ctx", 1)
    mixed, finish_back = jax.vjp(finish, carried, local_out, initial, gate_lin, head_gain)
    mixed_b = mixed.astype(jnp.bfloat16)
    mixer_part = jnp.einsum("rc,dc->rd", mixed_b, full_output, preferred_element_type=jnp.float32)
    attention = lax.psum(mixer_part.astype(jnp.bfloat16), "tp").astype(jnp.float32)
    middle = inputs + attention
    rms_two = lax.rsqrt(jnp.mean(middle * middle, -1, keepdims=True) + EPSILON)
    normed_two = middle * rms_two
    hidden_two = (normed_two * gain_two).astype(jnp.bfloat16)
    gate_up = jnp.dot(hidden_two, full_gate_up, preferred_element_type=jnp.float32)
    gate_pre = gate_up[:, :ff_cols]
    up_pre = gate_up[:, ff_cols:]
    sigma = jax.nn.sigmoid(gate_pre)
    swish = gate_pre * sigma
    activ = (swish * up_pre).astype(jnp.bfloat16)
    feed_part = jnp.einsum("rf,df->rd", activ, full_hidden_down, preferred_element_type=jnp.float32)
    grad_rows = cotangent.reshape(-1, width)
    grad_out = grad_rows.astype(jnp.float32)
    d_activ = jnp.dot(grad_rows, full_hidden_down, preferred_element_type=jnp.float32)
    d_gate_pre = (d_activ * up_pre * sigma * (1.0 + gate_pre * (1.0 - sigma))).astype(jnp.bfloat16)
    d_up_pre = (d_activ * swish).astype(jnp.bfloat16)
    grad_down = jnp.einsum("rd,rf->df", grad_rows, activ, preferred_element_type=jnp.float32)
    d_gate_up = jnp.concatenate([d_gate_pre, d_up_pre], 1)
    grad_gate_up = jnp.einsum(
        "rd,rf->df", hidden_two, d_gate_up, preferred_element_type=jnp.float32
    )
    two_part = jnp.einsum("rf,df->rd", d_gate_up, full_gate_up, preferred_element_type=jnp.float32)
    d_hidden_two = lax.psum(two_part.astype(jnp.bfloat16), "tp").astype(jnp.float32)
    grad_gain_two = jnp.sum(d_hidden_two * normed_two, 0)
    dn_two = d_hidden_two * gain_two
    d_middle = grad_out + rms_two * (
        dn_two - normed_two * jnp.mean(dn_two * normed_two, -1, keepdims=True)
    )
    d_middle_b = d_middle.astype(jnp.bfloat16)
    d_mixed = jnp.dot(d_middle_b, full_output, preferred_element_type=jnp.float32)
    grad_output = jnp.einsum("rd,rc->dc", d_middle_b, mixed_b, preferred_element_type=jnp.float32)
    d_carried, d_local, init_grad, d_gate, d_head = finish_back(d_mixed)
    transposed = jnp.transpose(transfer, (0, 2, 1))

    end_grad = jnp.zeros_like(offset)
    for _ in range(lax.axis_size("ctx") - 1):
        end_grad = passed_along(apply_map(transposed, init_grad, end_grad), "ctx", -1)
    d_transfer = mm("hdw,hew->hde", end_grad, initial)
    d_pre_ext, d_decay, d_beta, d_conv, d_log, d_bias = expand_back(
        (d_carried, d_local, d_transfer, end_grad)
    )
    edge_back = passed_along(d_pre_ext[:margin], "ctx", -1)
    own_grad = d_pre_ext[margin:]
    d_pre = jnp.concatenate(
        [own_grad[: row_count - margin], own_grad[row_count - margin :] + edge_back], 0
    )
    d_proj = jnp.concatenate(
        [d_pre, d_gate, d_decay, d_beta, jnp.zeros((row_count, 2 + pad_cols), jnp.float32)], 1
    ).astype(jnp.bfloat16)
    grad_input = jnp.einsum("rd,rc->dc", hidden_one, d_proj, preferred_element_type=jnp.float32)
    one_part = jnp.einsum("rc,dc->rd", d_proj, in_weights, preferred_element_type=jnp.float32)
    value_dim = d_head.shape[0]
    head_row = jnp.zeros((16, width), jnp.bfloat16)
    head_row = head_row.at[0, :value_dim].set(d_head.astype(jnp.bfloat16))
    one_sum = lax.psum(jnp.concatenate([one_part.astype(jnp.bfloat16), head_row], 0), "tp")
    one_sum = one_sum.astype(jnp.float32)
    d_hidden_one, head_sum = one_sum[:row_count], one_sum[row_count, :value_dim]
    feed = lax.psum(feed_part.astype(jnp.bfloat16), "tp").astype(jnp.float32)
    block_out = (middle + feed).astype(jnp.bfloat16).reshape(tokens.shape)
    grad_gain_one = jnp.sum(d_hidden_one * normed_one, 0)
    dn_one = d_hidden_one * gain_one
    tokens_grad = d_middle + rms_one * (
        dn_one - normed_one * jnp.mean(dn_one * normed_one, -1, keepdims=True)
    )
    tokens_grad = tokens_grad.reshape(tokens.shape)
    edges = [
        0,
        query_cols,
        2 * query_cols,
        conv_cols,
        conv_cols + value_cols,
        conv_cols + value_cols + head_count,
        conv_cols + value_cols + 2 * head_count,
    ]

    def scattered(member):
        total = lax.psum_scatter(
            member.astype(jnp.bfloat16), axes, scatter_dimension=0, tiled=True
        )
        return total.astype(jnp.float32)

    column = jnp.arange(grad_input.shape[1])[None, :]
    grad_input = jnp.where(column == used - 2, grad_gain_one[:, None], grad_input)
    grad_input = jnp.where(column == used - 1, grad_gain_two[:, None], grad_input)
    down_own = scattered(grad_down)
    gate_up_own = scattered(grad_gate_up)
    output_own = scattered(grad_output)
    input_own = scattered(grad_input)
    reduced = (
        input_own[:, used - 2],
        input_own[:, used - 1],
        *(input_own[:, edges[i] : edges[i + 1]] for i in range(6)),
        output_own,
        gate_up_own[:, :ff_cols],
        gate_up_own[:, ff_cols:],
        down_own,
    )
    conv_total, log_total, bias_total, head_total = lax.psum(
        (d_conv, d_log, d_bias, head_sum), ("dp", "ctx")
    )
    return (
        block_out,
        tokens_grad,
        reduced[0],
        reduced[1],
        reduced[2],
        reduced[3],
        reduced[4],
        reduced[5],
        reduced[6],
        reduced[7],
        reduced[8],
        conv_total[:, :query_cols],
        conv_total[:, query_cols : 2 * query_cols],
        conv_total[:, 2 * query_cols :],
        log_total,
        bias_total,
        head_total,
        reduced[9],
        reduced[10],
        reduced[11],
    )


def solution(mesh):
    return jax.shard_map(
        local,
        mesh=mesh,
        in_specs=(
            P("dp", "ctx", None),
            P("dp", None),
            P("dp", "ctx", None),
            P(("dp", "ctx")),
            P(("dp", "ctx")),
            P(("dp", "ctx"), "tp"),
            P(("dp", "ctx"), "tp"),
            P(("dp", "ctx"), "tp"),
            P(("dp", "ctx"), "tp"),
            P(("dp", "ctx"), "tp"),
            P(("dp", "ctx"), "tp"),
            P(("dp", "ctx"), "tp"),
            P(None, "tp"),
            P(None, "tp"),
            P(None, "tp"),
            P("tp"),
            P("tp"),
            P(),
            P(("dp", "ctx"), "tp"),
            P(("dp", "ctx"), "tp"),
            P(("dp", "ctx"), "tp"),
        ),
        out_specs=(
            P("dp", "ctx", None),
            P("dp", "ctx", None),
            P(("dp", "ctx")),
            P(("dp", "ctx")),
            P(("dp", "ctx"), "tp"),
            P(("dp", "ctx"), "tp"),
            P(("dp", "ctx"), "tp"),
            P(("dp", "ctx"), "tp"),
            P(("dp", "ctx"), "tp"),
            P(("dp", "ctx"), "tp"),
            P(("dp", "ctx"), "tp"),
            P(None, "tp"),
            P(None, "tp"),
            P(None, "tp"),
            P("tp"),
            P("tp"),
            P(),
            P(("dp", "ctx"), "tp"),
            P(("dp", "ctx"), "tp"),
            P(("dp", "ctx"), "tp"),
        ),
        check_vma=False,
    )
```

```python
from functools import partial

import jax
import jax.numpy as jnp
from jax import lax
from jax.experimental import pallas as pl
from jax.experimental.pallas import tpu as pltpu
from jax.sharding import PartitionSpec as P

GROUP = 64


EPSILON = 1e-06
HIGHEST = lax.Precision.HIGHEST
HIGH = lax.Precision.HIGH
LANES = 128


def peer_of(axes, sizes, distance):
    flat = 0
    total = 1
    for axis, size in zip(axes, sizes):
        flat = flat * size + lax.axis_index(axis)
        total = total * size
    other = lax.rem(flat + distance, total)
    where = {}
    for axis, size in reversed(list(zip(axes, sizes))):
        where[axis] = lax.rem(other, size)
        other = other // size
    return where


def greet(axes, sizes, peers):
    barrier = pltpu.get_barrier_semaphore()
    for distance in range(1, peers + 1):
        pl.semaphore_signal(
            barrier,
            inc=1,
            device_id=peer_of(axes, sizes, distance),
            device_id_type=pl.DeviceIdType.MESH,
        )
    pl.semaphore_wait(barrier, peers)


def sum_kernel(axis, size, x_ref, out_ref, parts, mine, got, send, recv, send_two, recv_two):
    peers = size - 1
    me = lax.axis_index(axis)
    rows = x_ref.shape[0] // size
    greet((axis,), (size,), peers)

    def block(index):
        return pl.ds(pl.multiple_of(index * rows, rows), rows)

    copies = []
    for distance in range(1, size):
        other = lax.rem(me + distance, size)
        copy = pltpu.make_async_remote_copy(
            src_ref=x_ref.at[block(other)],
            dst_ref=parts.at[distance - 1],
            send_sem=send.at[distance - 1],
            recv_sem=recv.at[distance - 1],
            device_id={axis: other},
            device_id_type=pl.DeviceIdType.MESH,
        )
        copy.start()
        copies.append(copy)
    total = x_ref[block(me)].astype(jnp.float32)
    for distance in range(1, size):
        copies[distance - 1].wait_recv()
        total = total + parts[distance - 1].astype(jnp.float32)
    total = total.astype(out_ref.dtype)
    mine[...] = total
    out_ref[block(me)] = total
    more = []
    for distance in range(1, size):
        copy = pltpu.make_async_remote_copy(
            src_ref=mine,
            dst_ref=got.at[distance - 1],
            send_sem=send_two.at[distance - 1],
            recv_sem=recv_two.at[distance - 1],
            device_id={axis: lax.rem(me + distance, size)},
            device_id_type=pl.DeviceIdType.MESH,
        )
        copy.start()
        more.append(copy)
    for distance in range(1, size):
        more[distance - 1].wait_recv()
        out_ref[block(lax.rem(me + size - distance, size))] = got[distance - 1]
    for copy in copies + more:
        copy.wait_send()


def summed(value, axis, call):
    size = lax.axis_size(axis)
    if size == 1:
        return value
    rows, cols = value.shape
    piece = (size - 1, rows // size, cols)
    sems = pltpu.SemaphoreType.DMA((size - 1,))
    return pl.pallas_call(
        partial(sum_kernel, axis, size),
        out_shape=jax.ShapeDtypeStruct(value.shape, value.dtype),
        in_specs=[pl.BlockSpec(memory_space=pltpu.VMEM)],
        out_specs=pl.BlockSpec(memory_space=pltpu.VMEM),
        scratch_shapes=[
            pltpu.VMEM(piece, value.dtype),
            pltpu.VMEM(piece[1:], value.dtype),
            pltpu.VMEM(piece, value.dtype),
            sems,
            sems,
            sems,
            sems,
        ],
        cost_estimate=pl.CostEstimate(
            flops=value.size * 40000, bytes_accessed=value.size * 300, transcendentals=0
        ),
        compiler_params=pltpu.CompilerParams(collective_id=call, has_side_effects=True),
        name=f"tp_sum_{call}",
    )(value)


def small_kernel(axes, sizes, peers, x_ref, out_ref, parts, send, recv):
    greet(axes, sizes, peers)
    copies = []
    for distance in range(1, peers + 1):
        copy = pltpu.make_async_remote_copy(
            src_ref=x_ref,
            dst_ref=parts.at[distance - 1],
            send_sem=send.at[distance - 1],
            recv_sem=recv.at[distance - 1],
            device_id=peer_of(axes, sizes, distance),
            device_id_type=pl.DeviceIdType.MESH,
        )
        copy.start()
        copies.append(copy)
    flat = 0
    for axis, size in zip(axes, sizes):
        flat = flat * size + lax.axis_index(axis)
    for copy in copies:
        copy.wait()
    parts[peers] = x_ref[...]
    total = jnp.zeros(x_ref.shape, jnp.float32)
    for owner in range(peers + 1):
        slot = lax.rem(flat + 2 * (peers + 1) - owner - 1, peers + 1)
        total = total + parts[slot]
    out_ref[...] = total


def small_sum(value, axes, call):
    sizes = tuple(lax.axis_size(axis) for axis in axes)
    peers = 1
    for size in sizes:
        peers = peers * size
    peers = peers - 1
    if peers == 0:
        return value
    return pl.pallas_call(
        partial(small_kernel, axes, sizes, peers),
        out_shape=jax.ShapeDtypeStruct(value.shape, value.dtype),
        in_specs=[pl.BlockSpec(memory_space=pltpu.VMEM)],
        out_specs=pl.BlockSpec(memory_space=pltpu.VMEM),
        scratch_shapes=[
            pltpu.VMEM((peers + 1,) + value.shape, value.dtype),
            pltpu.SemaphoreType.DMA((peers,)),
            pltpu.SemaphoreType.DMA((peers,)),
        ],
        cost_estimate=pl.CostEstimate(
            flops=1000000, bytes_accessed=20000000, transcendentals=0
        ),
        compiler_params=pltpu.CompilerParams(collective_id=call, has_side_effects=True),
        name=f"small_sum_{call}",
    )(value)


def passed_along(value, axis, by):
    devices = lax.axis_size(axis)
    pairs = [(i, i + by) for i in range(devices) if 0 <= i + by < devices]
    return lax.ppermute(value, axis, pairs)


def features(pre_ext, seg_ext, conv_weight, decay_lin, beta_lin, decay_log, decay_bias, key_dim):
    margin = conv_weight.shape[0] - 1
    row_count = pre_ext.shape[0] - margin
    head_count = decay_lin.shape[1]
    own_segment = seg_ext[margin:]
    convolved = jnp.zeros((row_count, pre_ext.shape[1]), jnp.float32)
    for lag in range(margin + 1):
        first_row = margin - lag
        same_doc = (seg_ext[first_row : first_row + row_count] == own_segment).astype(jnp.float32)
        convolved = (
            convolved
            + conv_weight[lag][None, :]
            * pre_ext[first_row : first_row + row_count]
            * same_doc[:, None]
        )
    activated = jax.nn.silu(convolved)
    query_cols = head_count * key_dim
    queries = activated[:, :query_cols].reshape(row_count, head_count, key_dim)
    key_rows = activated[:, query_cols : 2 * query_cols].reshape(row_count, head_count, key_dim)
    value_rows = activated[:, 2 * query_cols :].reshape(row_count, head_count, -1)
    queries = (
        queries
        * lax.rsqrt(jnp.sum(queries * queries, -1, keepdims=True) + EPSILON)
        * key_dim ** (-0.5)
    )
    key_rows = key_rows * lax.rsqrt(jnp.sum(key_rows * key_rows, -1, keepdims=True) + EPSILON)
    decay_rate = -jnp.exp(decay_log)[None, :] * jax.nn.softplus(decay_lin + decay_bias[None, :])
    beta_gate = jax.nn.sigmoid(beta_lin)
    starts = (own_segment != seg_ext[margin - 1 : margin - 1 + row_count]).astype(jnp.float32)
    return (queries, key_rows, value_rows, decay_rate, beta_gate, starts)


def lower_inverse_value(lower_part):
    order = lower_part.shape[-1]
    negated = -lower_part
    inverse = jnp.eye(order, dtype=jnp.float32)[None] + negated
    power = negated
    span = 2
    while span < order:
        power = jnp.einsum("bij,bjk->bik", power, power, precision=HIGHEST)
        inverse = inverse + jnp.einsum("bij,bjk->bik", inverse, power, precision=HIGHEST)
        span = span * 2
    return inverse


@jax.custom_vjp
def unit_lower_inverse(lower_part):
    return lower_inverse_value(lower_part)


def inverse_forward(lower_part):
    inverse = lower_inverse_value(lower_part)
    return inverse, inverse


def inverse_backward(inverse, grad):
    half = jnp.einsum("bji,bjk->bik", inverse, grad, precision=HIGHEST)
    return (-jnp.einsum("bij,bkj->bik", half, inverse, precision=HIGHEST),)


unit_lower_inverse.defvjp(inverse_forward, inverse_backward)


def mm(spec, left, right):
    return jnp.einsum(spec, left, right, precision=HIGH)


def group_maps(queries, key_rows, value_rows, decay_rate, beta_gate, starts, group):
    row_count, head_count, key_dim = queries.shape
    blocks = row_count // group

    def batched(member):
        tail = member.shape[2:]
        split = member.reshape((blocks, group, head_count) + tail)
        moved = jnp.moveaxis(split, 2, 1)
        return moved.reshape((blocks * head_count, group) + tail)

    queries, key_rows, value_rows = batched(queries), batched(key_rows), batched(value_rows)
    position = jnp.arange(group)
    until = (position[None, :] <= position[:, None]).astype(jnp.float32)
    beta = batched(beta_gate)
    cumulative = jnp.einsum("ts,bs->bt", until, batched(decay_rate), precision=HIGHEST)
    counted = jnp.cumsum(starts.reshape(blocks, group), axis=1)
    counted = jnp.broadcast_to(counted[:, None, :], (blocks, head_count, group))
    counted = counted.reshape(blocks * head_count, group)
    same_doc = (counted[:, :, None] == counted[:, None, :]) & (
        position[None, None, :] <= position[None, :, None]
    )
    same_value = same_doc.astype(jnp.float32)
    strictly = same_value * (position[None, :] < position[:, None]).astype(jnp.float32)[None]
    spread = cumulative[:, :, None] - cumulative[:, None, :]
    decay_pair = jnp.exp(jnp.where(same_doc, spread, 0.0)) * same_value
    anchor = jnp.exp(cumulative) * (counted == 0).astype(jnp.float32)
    closing = decay_pair[:, group - 1, :]
    key_gram = mm("btd,bjd->btj", key_rows, key_rows)
    inverse = unit_lower_inverse(beta[:, :, None] * decay_pair * key_gram * strictly)
    right = beta[:, :, None] * jnp.concatenate([-anchor[:, :, None] * key_rows, value_rows], 2)
    updates = mm("btj,bjw->btw", inverse, right)
    query_key = mm("btd,bjd->btj", queries, key_rows) * decay_pair
    from_rows = mm("btj,bjw->btw", query_key, updates)
    carried = from_rows[:, :, :key_dim] + anchor[:, :, None] * queries
    local_out = from_rows[:, :, key_dim:]
    maps = mm("bjd,bjw->bdw", key_rows * closing[:, :, None], updates)
    last = anchor[:, group - 1]
    transfer = maps[:, :, :key_dim] + last[:, None, None] * jnp.eye(key_dim, dtype=jnp.float32)
    offset = maps[:, :, key_dim:]

    def grouped(member):
        return member.reshape((blocks, head_count) + member.shape[1:])

    return grouped(carried), grouped(local_out), grouped(transfer), grouped(offset)


def compose(carried, local_out, transfer, offset):
    blocks = carried.shape[0]
    key_dim = carried.shape[-1]
    running = jnp.concatenate([transfer[0], offset[0]], 2)
    before = []
    for block in range(1, blocks):
        before.append(running)
        running = mm("hde,hew->hdw", transfer[block], running)
        running = jnp.concatenate(
            [running[:, :, :key_dim], running[:, :, key_dim:] + offset[block]], 2
        )
    if blocks > 1:
        mixed_in = mm("ghtd,ghdw->ghtw", carried[1:], jnp.stack(before))
        carried = jnp.concatenate([carried[:1], mixed_in[..., :key_dim]], 0)
        local_out = jnp.concatenate(
            [local_out[:1], local_out[1:] + mixed_in[..., key_dim:]], 0
        )
    return carried, local_out, running[:, :, :key_dim], running[:, :, key_dim:]


def gated(output_rows, gate_lin, head_gain):
    row_count, head_count, value_dim = output_rows.shape
    scaled = output_rows * lax.rsqrt(
        jnp.mean(output_rows * output_rows, -1, keepdims=True) + EPSILON
    )
    gate_rows = gate_lin.reshape(row_count, head_count, value_dim)
    return (scaled * head_gain * jax.nn.silu(gate_rows)).reshape(row_count, head_count * value_dim)


def expand(
    pre_ext, decay_lin, beta_lin, conv_weight, decay_log, decay_bias, seg_ext, key_dim, group
):
    queries, key_rows, value_rows, decay_rate, beta_gate, starts = features(
        pre_ext, seg_ext, conv_weight, decay_lin, beta_lin, decay_log, decay_bias, key_dim
    )
    return compose(
        *group_maps(queries, key_rows, value_rows, decay_rate, beta_gate, starts, group)
    )


def finish(carried, local_out, initial, gate_lin, head_gain):
    output_rows = local_out + mm("ghtd,hdw->ghtw", carried, initial)
    blocks, head_count, group, value_dim = output_rows.shape
    output_rows = jnp.transpose(output_rows, (0, 2, 1, 3)).reshape(
        blocks * group, head_count, value_dim
    )
    return gated(output_rows, gate_lin, head_gain)


def apply_map(matrix, addend, incoming):
    return mm("hde,hew->hdw", matrix, incoming) + addend


def local(
    tokens,
    segments,
    cotangent,
    mixer_gain,
    mlp_gain,
    query_weight,
    key_weight,
    value_weight,
    gate_weight,
    decay_weight,
    beta_weight,
    output_weight,
    conv_query,
    conv_key,
    conv_value,
    decay_log,
    decay_bias,
    head_gain,
    hidden_gate,
    hidden_up,
    hidden_down,
):
    width = tokens.shape[-1]
    inputs = tokens.reshape(-1, width).astype(jnp.float32)
    row_count = inputs.shape[0]
    query_cols = query_weight.shape[1]
    value_cols = value_weight.shape[1]
    head_count = decay_weight.shape[1]
    ff_cols = hidden_gate.shape[1]
    axes = ("dp", "ctx")
    used = 2 * query_cols + 2 * value_cols + 2 * head_count + 2
    pad_cols = -used % LANES
    own_rows = query_weight.shape[0]
    in_weights = lax.all_gather(
        jnp.concatenate(
            [
                query_weight,
                key_weight,
                value_weight,
                gate_weight,
                decay_weight,
                beta_weight,
                mixer_gain[:, None],
                mlp_gain[:, None],
                jnp.zeros((own_rows, pad_cols), jnp.bfloat16),
            ],
            1,
        ),
        axes,
        axis=0,
        tiled=True,
    )
    full_output = lax.all_gather(output_weight, axes, axis=0, tiled=True)
    full_gate_up = lax.all_gather(
        jnp.concatenate([hidden_gate, hidden_up], 1), axes, axis=0, tiled=True
    )
    full_hidden_down = lax.all_gather(hidden_down, axes, axis=0, tiled=True)
    gain_one = in_weights[:, used - 2].astype(jnp.float32)
    gain_two = in_weights[:, used - 1].astype(jnp.float32)
    conv_cols = 2 * query_cols + value_cols
    key_dim = query_cols // head_count
    rms_one = lax.rsqrt(jnp.mean(inputs * inputs, -1, keepdims=True) + EPSILON)
    normed_one = inputs * rms_one
    hidden_one = (normed_one * gain_one).astype(jnp.bfloat16)
    projected = jnp.dot(hidden_one, in_weights, preferred_element_type=jnp.float32)
    pre_conv = projected[:, :conv_cols].astype(jnp.bfloat16)
    gate_lin = projected[:, conv_cols : conv_cols + value_cols]
    decay_lin = projected[:, conv_cols + value_cols : conv_cols + value_cols + head_count]
    beta_lin = projected[:, used - 2 - head_count : used - 2]
    conv_weight = jnp.concatenate([conv_query, conv_key, conv_value], 1)
    margin = conv_weight.shape[0] - 1
    edge_rows = passed_along(pre_conv[row_count - margin :], "ctx", 1)
    pre_ext = jnp.concatenate([edge_rows, pre_conv], 0).astype(jnp.float32)
    seg_padded = jnp.concatenate([jnp.full((margin,), -1, jnp.int32), segments.reshape(-1)], 0)
    seg_ext = lax.dynamic_slice_in_dim(
        seg_padded, lax.axis_index("ctx") * row_count, row_count + margin
    )
    expand_fn = partial(expand, seg_ext=seg_ext, key_dim=key_dim, group=GROUP)
    (carried, local_out, transfer, offset), expand_back = jax.vjp(
        expand_fn, pre_ext, decay_lin, beta_lin, conv_weight, decay_log, decay_bias
    )

    initial = jnp.zeros_like(offset)
    for _ in range(lax.axis_size("ctx") - 1):
        initial = passed_along(apply_map(transfer, offset, initial), "ctx", 1)
    mixed, finish_back = jax.vjp(finish, carried, local_out, initial, gate_lin, head_gain)
    mixed_b = mixed.astype(jnp.bfloat16)
    mixer_part = jnp.einsum("rc,dc->rd", mixed_b, full_output, preferred_element_type=jnp.float32)
    attention = summed(mixer_part.astype(jnp.bfloat16), "tp", 0).astype(jnp.float32)
    middle = inputs + attention
    rms_two = lax.rsqrt(jnp.mean(middle * middle, -1, keepdims=True) + EPSILON)
    normed_two = middle * rms_two
    hidden_two = (normed_two * gain_two).astype(jnp.bfloat16)
    gate_up = jnp.dot(hidden_two, full_gate_up, preferred_element_type=jnp.float32)
    gate_pre = gate_up[:, :ff_cols]
    up_pre = gate_up[:, ff_cols:]
    sigma = jax.nn.sigmoid(gate_pre)
    swish = gate_pre * sigma
    activ = (swish * up_pre).astype(jnp.bfloat16)
    feed_part = jnp.einsum("rf,df->rd", activ, full_hidden_down, preferred_element_type=jnp.float32)
    grad_rows = cotangent.reshape(-1, width)
    grad_out = grad_rows.astype(jnp.float32)
    d_activ = jnp.dot(grad_rows, full_hidden_down, preferred_element_type=jnp.float32)
    d_gate_pre = (d_activ * up_pre * sigma * (1.0 + gate_pre * (1.0 - sigma))).astype(jnp.bfloat16)
    d_up_pre = (d_activ * swish).astype(jnp.bfloat16)
    grad_down = jnp.einsum("rd,rf->df", grad_rows, activ, preferred_element_type=jnp.float32)
    d_gate_up = jnp.concatenate([d_gate_pre, d_up_pre], 1)
    grad_gate_up = jnp.einsum(
        "rd,rf->df", hidden_two, d_gate_up, preferred_element_type=jnp.float32
    )
    two_part = jnp.einsum("rf,df->rd", d_gate_up, full_gate_up, preferred_element_type=jnp.float32)
    both = summed(jnp.concatenate([two_part, feed_part], 0).astype(jnp.bfloat16), "tp", 1)
    d_hidden_two = both[:row_count].astype(jnp.float32)
    feed = both[row_count:].astype(jnp.float32)
    block_out = (middle + feed).astype(jnp.bfloat16).reshape(tokens.shape)

    def scattered(member):
        total = lax.psum_scatter(
            member.astype(jnp.bfloat16), axes, scatter_dimension=0, tiled=True
        )
        return total.astype(jnp.float32)

    down_own = scattered(grad_down)
    gate_up_own = scattered(grad_gate_up)
    grad_gain_two = jnp.sum(d_hidden_two * normed_two, 0)
    dn_two = d_hidden_two * gain_two
    d_middle = grad_out + rms_two * (
        dn_two - normed_two * jnp.mean(dn_two * normed_two, -1, keepdims=True)
    )
    d_middle_b = d_middle.astype(jnp.bfloat16)
    d_mixed = jnp.dot(d_middle_b, full_output, preferred_element_type=jnp.float32)
    grad_output = jnp.einsum("rd,rc->dc", d_middle_b, mixed_b, preferred_element_type=jnp.float32)
    d_carried, d_local, init_grad, d_gate, d_head = finish_back(d_mixed)
    transposed = jnp.transpose(transfer, (0, 2, 1))

    end_grad = jnp.zeros_like(offset)
    for _ in range(lax.axis_size("ctx") - 1):
        end_grad = passed_along(apply_map(transposed, init_grad, end_grad), "ctx", -1)
    d_transfer = mm("hdw,hew->hde", end_grad, initial)
    d_pre_ext, d_decay, d_beta, d_conv, d_log, d_bias = expand_back(
        (d_carried, d_local, d_transfer, end_grad)
    )
    edge_back = passed_along(d_pre_ext[:margin], "ctx", -1)
    own_grad = d_pre_ext[margin:]
    d_pre = jnp.concatenate(
        [own_grad[: row_count - margin], own_grad[row_count - margin :] + edge_back], 0
    )
    d_proj = jnp.concatenate(
        [d_pre, d_gate, d_decay, d_beta, jnp.zeros((row_count, 2 + pad_cols), jnp.float32)], 1
    ).astype(jnp.bfloat16)
    grad_input = jnp.einsum("rd,rc->dc", hidden_one, d_proj, preferred_element_type=jnp.float32)
    one_part = jnp.einsum("rc,dc->rd", d_proj, in_weights, preferred_element_type=jnp.float32)
    one_part, down_own = lax.optimization_barrier((one_part, down_own))
    one_sum = summed(one_part.astype(jnp.bfloat16), "tp", 2)
    one_sum, gate_up_own = lax.optimization_barrier((one_sum, gate_up_own))
    d_hidden_one = one_sum.astype(jnp.float32)
    grad_gain_one = jnp.sum(d_hidden_one * normed_one, 0)
    dn_one = d_hidden_one * gain_one
    tokens_grad = d_middle + rms_one * (
        dn_one - normed_one * jnp.mean(dn_one * normed_one, -1, keepdims=True)
    )
    tokens_grad = tokens_grad.reshape(tokens.shape)
    edges = [
        0,
        query_cols,
        2 * query_cols,
        conv_cols,
        conv_cols + value_cols,
        conv_cols + value_cols + head_count,
        conv_cols + value_cols + 2 * head_count,
    ]

    column = jnp.arange(grad_input.shape[1])[None, :]
    grad_input = jnp.where(column == used - 2, grad_gain_one[:, None], grad_input)
    grad_input = jnp.where(column == used - 1, grad_gain_two[:, None], grad_input)
    output_own = scattered(grad_output)
    input_own = scattered(grad_input)
    reduced = (
        input_own[:, used - 2],
        input_own[:, used - 1],
        *(input_own[:, edges[i] : edges[i + 1]] for i in range(6)),
        output_own,
        gate_up_own[:, :ff_cols],
        gate_up_own[:, ff_cols:],
        down_own,
    )
    taps, conv_width = d_conv.shape
    value_dim = d_head.shape[0]
    rest = jnp.concatenate([d_head, d_log, d_bias])
    pad_row = jnp.zeros((-rest.shape[0] % conv_width,), jnp.float32)
    rest = jnp.concatenate([rest, pad_row]).reshape(-1, conv_width)
    packed = jnp.concatenate([d_conv, rest], 0)
    lines = packed.shape[0]
    packed = jnp.concatenate([packed, jnp.zeros((-lines % 8, conv_width), jnp.float32)], 0)
    packed = small_sum(packed, ("dp", "ctx"), 3)
    conv_total = packed[:taps]
    rest = packed[taps:lines].reshape(-1)
    log_total = rest[value_dim : value_dim + head_count]
    bias_total = rest[value_dim + head_count : value_dim + 2 * head_count]
    head_total = small_sum(
        jnp.broadcast_to(rest[None, :value_dim], (8, value_dim)), ("tp",), 4
    )[0]
    return (
        block_out,
        tokens_grad,
        reduced[0],
        reduced[1],
        reduced[2],
        reduced[3],
        reduced[4],
        reduced[5],
        reduced[6],
        reduced[7],
        reduced[8],
        conv_total[:, :query_cols],
        conv_total[:, query_cols : 2 * query_cols],
        conv_total[:, 2 * query_cols :],
        log_total,
        bias_total,
        head_total,
        reduced[9],
        reduced[10],
        reduced[11],
    )


def solution(mesh):
    return jax.shard_map(
        local,
        mesh=mesh,
        in_specs=(
            P("dp", "ctx", None),
            P("dp", None),
            P("dp", "ctx", None),
            P(("dp", "ctx")),
            P(("dp", "ctx")),
            P(("dp", "ctx"), "tp"),
            P(("dp", "ctx"), "tp"),
            P(("dp", "ctx"), "tp"),
            P(("dp", "ctx"), "tp"),
            P(("dp", "ctx"), "tp"),
            P(("dp", "ctx"), "tp"),
            P(("dp", "ctx"), "tp"),
            P(None, "tp"),
            P(None, "tp"),
            P(None, "tp"),
            P("tp"),
            P("tp"),
            P(),
            P(("dp", "ctx"), "tp"),
            P(("dp", "ctx"), "tp"),
            P(("dp", "ctx"), "tp"),
        ),
        out_specs=(
            P("dp", "ctx", None),
            P("dp", "ctx", None),
            P(("dp", "ctx")),
            P(("dp", "ctx")),
            P(("dp", "ctx"), "tp"),
            P(("dp", "ctx"), "tp"),
            P(("dp", "ctx"), "tp"),
            P(("dp", "ctx"), "tp"),
            P(("dp", "ctx"), "tp"),
            P(("dp", "ctx"), "tp"),
            P(("dp", "ctx"), "tp"),
            P(None, "tp"),
            P(None, "tp"),
            P(None, "tp"),
            P("tp"),
            P("tp"),
            P(),
            P(("dp", "ctx"), "tp"),
            P(("dp", "ctx"), "tp"),
            P(("dp", "ctx"), "tp"),
        ),
        check_vma=False,
    )
```
